32 devices in a mesh: ctx: 8 (over z, x), tp: 4 (over y, core).
Axes of the slice: x: 2, y: 2, z: 4, core: 2. Of those that a mesh axis runs over, the one named last changes fastest.
Arguments:
- q_raw: bfloat16 [2048, 4096], P('ctx', 'tp'), may hold values from -36 to 36
- k_raw: bfloat16 [2048, 2048], P('ctx', 'tp'), may hold values from -36 to 36
- v_cur: bfloat16 [2048, 2048], P('ctx', 'tp'), may hold values from -6 to 6
- d_out: bfloat16 [2048, 4096], P('ctx', 'tp'), may hold values from -6 to 6
- q_gain: float32 [128], replicated, may hold values from 0.25 to 1.75
- k_gain: float32 [128], replicated, may hold values from 0.25 to 1.75
Outputs:
- dq_raw: bfloat16 [2048, 4096], P('ctx', 'tp')
- dk_raw: bfloat16 [2048, 2048], P('ctx', 'tp')
- dv: bfloat16 [2048, 2048], P('ctx', 'tp')
- q_gain_grad: float32 [128], replicated
- k_gain_grad: float32 [128], replicated
The draws below stay inside these ranges and needn't reach their ends.
All inputs are finite; a program needn't handle non-finite values.
Results may differ from the reference program's by a relative error of at most 0.0077.
Values may be sent and summed in bfloat16 or wider, within the bound.
A program may use at most 64 MiB of HBM per device.

```python
import jax
import jax.numpy as jnp
from jax import lax

Q_HEADS = 32
KV_HEADS = 16
HEAD_DIM = 128
WINDOW = 1024
TOK_DEV = 256
HOPS = 4
TOKENS = 2048


def scaled_entries(key, row_count, col_count):
    first, second, third = jax.random.split(key, 3)
    base = jax.random.truncated_normal(first, -4.0, 4.0, (row_count, col_count), jnp.float32)
    row_scale = jnp.exp(jax.random.uniform(second, (row_count, 1), jnp.float32, -1.2039728, 1.0986123))
    col_scale = jnp.exp(jax.random.uniform(third, (1, col_count), jnp.float32, -1.2039728, 1.0986123))
    return base * row_scale * col_scale


def draw_q_raw(key, part):
    return scaled_entries(jax.random.fold_in(key, 11), TOKENS, Q_HEADS * HEAD_DIM).astype(jnp.bfloat16)


def draw_k_raw(key, part):
    return scaled_entries(jax.random.fold_in(key, 23), TOKENS, KV_HEADS * HEAD_DIM).astype(jnp.bfloat16)


def level_of(key, shape, shards, smallest, largest):
    def one(dim, blocks):
        draws = jax.random.uniform(jax.random.fold_in(jax.random.fold_in(key, 6), dim), (blocks,), jnp.float32, smallest / len(shards), largest / len(shards))
        return jnp.repeat(jnp.exp(draws), shape[dim] // blocks).reshape((-1,) + (1,) * (len(shape) - dim - 1))

    loudness = one(*shards[0])
    for cut in shards[1:]:
        loudness = loudness * one(*cut)
    return loudness


def scatter_about(stream_key, extent, spread, reach, pieces=(), kind=jnp.bfloat16):
    array = spread * jax.random.normal(stream_key, extent, jnp.float32)
    if pieces:
        array = array * level_of(stream_key, extent, pieces, -0.22, 0.18)
    return jnp.clip(array, -reach, reach).astype(kind)


def setup_inputs(seed: int = 0) -> dict:
    key_list = jax.random.split(jax.random.key(seed), 7)
    return {
        "q_raw": draw_q_raw(jax.random.fold_in(key_list[6], 71), 0),
        "k_raw": draw_k_raw(jax.random.fold_in(key_list[6], 71), 0),
        "v_cur": scatter_about(key_list[2], (TOKENS, KV_HEADS * HEAD_DIM), 1.0, 6.0, ((0, 8), (1, 4))),
        "d_out": scatter_about(key_list[3], (TOKENS, Q_HEADS * HEAD_DIM), 1.0, 6.0, ((0, 8), (1, 4))),
        "q_gain": jnp.clip(1.0 + 0.15 * jax.random.normal(key_list[4], (HEAD_DIM,), jnp.float32), 0.25, 1.75),
        "k_gain": jnp.clip(1.0 + 0.15 * jax.random.normal(key_list[5], (HEAD_DIM,), jnp.float32), 0.25, 1.75),
    }


score_scale = 168.0 ** (-0.5)
epsilon = 1e-06

def normalize(raw32, gain):
    vectors = raw32.reshape(raw32.shape[0], -1, HEAD_DIM)
    inverse = lax.rsqrt(lax.optimization_barrier(jnp.mean(vectors * vectors, axis=-1, keepdims=True)) + epsilon)
    return vectors * inverse * gain

def rounded_terms(block):
    low = lax.optimization_barrier(block.astype(jnp.bfloat16)).astype(jnp.float32)
    return low.reshape(HOPS + 1, TOK_DEV, KV_HEADS, HEAD_DIM)

def reference(q_raw, k_raw, v_cur, d_out, q_gain, k_gain):
    q32 = q_raw.astype(jnp.float32)
    k32 = k_raw.astype(jnp.float32)
    q_normed, pull_query = jax.vjp(normalize, q32, q_gain)
    k_normed, pull_key = jax.vjp(normalize, k32, k_gain)
    q_low = q_normed.astype(jnp.bfloat16)
    k_low = k_normed.astype(jnp.bfloat16)
    group = Q_HEADS // KV_HEADS
    block_count = TOKENS // TOK_DEV
    band_width = WINDOW + TOK_DEV
    query_blocks = q_low.reshape(block_count, TOK_DEV, KV_HEADS, group, HEAD_DIM)
    grad_blocks = d_out.reshape(block_count, TOK_DEV, KV_HEADS, group, HEAD_DIM)
    value_low = v_cur.reshape(TOKENS, KV_HEADS, HEAD_DIM)
    key_padded = jnp.concatenate([jnp.zeros_like(k_low[:WINDOW]), k_low], axis=0)
    value_padded = jnp.concatenate([jnp.zeros_like(value_low[:WINDOW]), value_low], axis=0)
    row_ids = lax.broadcasted_iota(jnp.int32, (TOK_DEV, band_width), 0)
    col_ids = lax.broadcasted_iota(jnp.int32, (TOK_DEV, band_width), 1)
    distance = row_ids + WINDOW - col_ids
    base_visible = (distance >= 0) & (distance < WINDOW)

    def one_block(block_index):
        start = (block_index * TOK_DEV).astype(jnp.int32)
        band_keys = lax.dynamic_slice_in_dim(key_padded, start, band_width, 0).astype(jnp.float32)
        band_values = lax.dynamic_slice_in_dim(value_padded, start, band_width, 0).astype(jnp.float32)
        queries = lax.dynamic_index_in_dim(query_blocks, block_index, 0, keepdims=False).astype(jnp.float32)
        grads = lax.dynamic_index_in_dim(grad_blocks, block_index, 0, keepdims=False).astype(jnp.float32)
        visible = base_visible & (start - WINDOW + col_ids >= 0)
        scores = jnp.einsum('tkgd,ckd->kgtc', queries, band_keys) * score_scale
        exp_scores = jnp.where(visible, jnp.exp(scores), 0.0)
        probs = exp_scores / lax.optimization_barrier(jnp.sum(exp_scores, axis=-1, keepdims=True))
        dprobs = jnp.einsum('tkgd,ckd->kgtc', grads, band_values)
        row_delta = lax.optimization_barrier(jnp.sum(probs * dprobs, axis=-1, keepdims=True))
        dscores = lax.optimization_barrier((probs * (dprobs - row_delta) * score_scale).astype(jnp.bfloat16)).astype(jnp.float32)
        probs_low = lax.optimization_barrier(probs.astype(jnp.bfloat16)).astype(jnp.float32)
        dq_block = jnp.einsum('kgtc,ckd->tkgd', dscores, band_keys)
        dk_block = rounded_terms(jnp.einsum('kgtc,tkgd->ckd', dscores, queries))
        dv_block = rounded_terms(jnp.einsum('kgtc,tkgd->ckd', probs_low, grads))
        return (dq_block, dk_block, dv_block)
    dq_all, dk_all, dv_all = lax.map(one_block, jnp.arange(block_count, dtype=jnp.int32))

    def intersection_add(terms):
        total = jnp.zeros((block_count, TOK_DEV, KV_HEADS, HEAD_DIM), jnp.float32)
        for segment in range(HOPS + 1):
            lag = HOPS - segment
            part = terms[:, segment]
            shifted = jnp.concatenate([part[lag:], jnp.zeros_like(part[:lag])], axis=0)
            total = total + shifted
        return total.reshape(TOKENS, KV_HEADS, HEAD_DIM)
    key_grad = intersection_add(dk_all)
    value_grad = intersection_add(dv_all)
    query_grad = dq_all.reshape(TOKENS, Q_HEADS, HEAD_DIM)
    dq_raw32, q_gain_total = pull_query(query_grad)
    dk_raw32, k_gain_total = pull_key(key_grad)
    dq_raw = dq_raw32.reshape(TOKENS, -1).astype(jnp.bfloat16)
    dk_raw = dk_raw32.reshape(TOKENS, -1).astype(jnp.bfloat16)
    dv = value_grad.reshape(TOKENS, -1).astype(jnp.bfloat16)
    q_gain_grad = (q_gain_total / jnp.sqrt(jnp.float32(TOKENS * Q_HEADS))).astype(jnp.float32)
    k_gain_grad = (k_gain_total / jnp.sqrt(jnp.float32(TOKENS * KV_HEADS))).astype(jnp.float32)
    return (dq_raw, dk_raw, dv, q_gain_grad, k_gain_grad)
```

```python
import functools

import jax
import jax.numpy as jnp
from jax import lax
from jax.experimental import pallas as pl
from jax.experimental.pallas import tpu as pltpu
from jax.sharding import PartitionSpec as P

Q_HEADS = 32
KV_HEADS = 16
HEAD_DIM = 128
WINDOW = 1024

score_scale = 168.0 ** (-0.5)
epsilon = 1e-06
MESH = pl.DeviceIdType.MESH
F32 = jnp.float32
BF16 = jnp.bfloat16
T = 256
D = HEAD_DIM
BLOCKS = 5


def nt(a, b):
    return lax.dot_general(a, b, (((1,), (1,)), ((), ())), preferred_element_type=F32)


def tn(a, b):
    return lax.dot_general(a, b, (((0,), (0,)), ((), ())), preferred_element_type=F32)


def inverse_norm(x):
    return lax.rsqrt(jnp.mean(x * x, axis=-1, keepdims=True) + epsilon)


def norm_back(x, inv, gain, grad):
    unit = x * inv
    pulled = grad * gain
    raw = inv * (pulled - unit * jnp.mean(pulled * unit, axis=-1, keepdims=True))
    return raw, jnp.sum(grad * unit, axis=0, keepdims=True)


def kernel(n, m, q_in, k_in, v_in, g_in, qg, kg, dq_o, dk_o, dv_o, gain_o,
           q_b, g_b, k_b, v_b, kv, e_b, d_b, l_b, delta_b, dqt, acc, term, got, dq_s, dk_s, dv_s,
           gain_acc, gain_c, gain_t,
           x_loc, x_snd, x_rcv, f_snd, f_rcv, b_snd, b_rcv, o_loc, o_snd, o_rcv,
           p_loc, p_snd, p_rcv, c_snd, c_rcv, t_snd, t_rcv):
    c = lax.axis_index("ctx")
    tp = lax.axis_index("tp")
    x = lax.rem(c, 2)
    xp = c + 1 - 2 * x
    up = {"ctx": c + 2}
    down = {"ctx": c - 2}
    side = {"ctx": xp}
    has_next = c + 2 < n
    has_prev = c >= 2
    has_prev2 = c >= 4

    barrier = pltpu.get_barrier_semaphore()
    for k in range(1, n):
        pl.semaphore_signal(barrier, inc=1, device_id={"ctx": lax.rem(c + k, n)}, device_id_type=MESH)
    for k in range(1, m):
        pl.semaphore_signal(barrier, inc=1, device_id={"tp": lax.rem(tp + k, m)}, device_id_type=MESH)
    pl.semaphore_wait(barrier, n - 1 + m - 1)

    def remote(src, dst, snd, rcv, to):
        return pltpu.make_async_remote_copy(src_ref=src, dst_ref=dst, send_sem=snd, recv_sem=rcv,
                                            device_id=to, device_id_type=MESH)

    mine = pl.ds(pl.multiple_of(x * T, T), T)
    swaps = []
    for i, (src, dst, width) in enumerate(((k_in, k_b, 2 * D), (v_in, v_b, 2 * D), (q_in, q_b, 4 * D), (g_in, g_b, 4 * D))):
        there = pl.ds(pl.multiple_of((1 - x) * width, width), width)
        here = pl.ds(pl.multiple_of(x * width, width), width)
        far = remote(src.at[:, there], dst.at[mine, :], x_snd.at[i], x_rcv.at[i], side)
        near = pltpu.make_async_copy(src.at[:, here], dst.at[mine, :], x_loc.at[i])
        far.start()
        near.start()
        swaps.append((far, near))

    gain_acc[...] = jnp.zeros_like(gain_acc)
    acc[...] = jnp.zeros_like(acc)
    for far, near in swaps[:2]:
        near.wait()
        far.wait_recv()
    own = pl.ds(4 * T, 2 * T)
    one = pl.ds(2 * T, 2 * T)
    two = pl.ds(0, 2 * T)

    def send_own(h):
        return remote(kv.at[h, :, own], kv.at[h, :, one], f_snd.at[h, 0], f_rcv.at[h, 0], up)

    def send_on(h):
        return remote(kv.at[h, :, one], kv.at[h, :, two], f_snd.at[h, 1], f_rcv.at[h, 1], up)

    def back_two(h):
        return remote(term.at[h, 0], got.at[h, 0], b_snd.at[h, 0], b_rcv.at[h, 0], down)

    def back_one(h):
        return remote(term.at[h, 1], got.at[h, 1], b_snd.at[h, 1], b_rcv.at[h, 1], down)

    def forward(h):
        @pl.when(has_prev)
        def _():
            send_own(h).wait_recv()

        @pl.when(has_prev & has_next)
        def _():
            send_on(h).start()

    for h in range(2):
        cols = slice(h * D, (h + 1) * D)
        raw = k_b[:, cols].astype(F32)
        kv[h, 0, 4 * T : 6 * T, :] = (raw * inverse_norm(raw) * kg[...]).astype(BF16)
        kv[h, 1, 4 * T : 6 * T, :] = v_b[:, cols]
        if h == 0:
            @pl.when(has_next)
            def _():
                send_own(0).start()

    forward(0)

    @pl.when(has_next)
    def _():
        send_own(1).start()

    for far, near in swaps[2:]:
        near.wait()
        far.wait_recv()

    row = lax.broadcasted_iota(jnp.int32, (T, 2 * T), 0)
    col = lax.rem(lax.broadcasted_iota(jnp.int32, (T, 2 * T), 1), T)

    def attend(s):
        h = s // 2
        qb = lax.rem(s, 2)
        rows = pl.ds(pl.multiple_of(qb * T, T), T)
        col0 = pl.ds(pl.multiple_of(h * 2 * D, D), D)
        col1 = pl.ds(pl.multiple_of(h * 2 * D + D, D), D)
        raw = jnp.concatenate([q_b[rows, col0], q_b[rows, col1]], axis=0).astype(F32)
        grads = jnp.concatenate([g_b[rows, col0], g_b[rows, col1]], axis=0)
        inv = inverse_norm(raw)
        queries = (raw * inv * qg[...]).astype(BF16)
        l_b[...] = jnp.zeros_like(l_b)
        delta_b[...] = jnp.zeros_like(delta_b)
        dqt[...] = jnp.zeros_like(dqt)

        def keyed(i, body):
            start = pl.multiple_of((qb + i) * T, T)
            if i == BLOCKS - 1:
                body(i, pl.ds(start, T))
            else:
                @pl.when(c - x - 4 + qb + i >= 0)
                def _():
                    body(i, pl.ds(start, T))

        def first(i, keys):
            scores = nt(kv[h, 0, keys, :], queries)
            e = jnp.exp(scores * score_scale)
            if i == 0:
                e = jnp.where(col < row, e, 0.0)
            if i == BLOCKS - 1:
                e = jnp.where(col >= row, e, 0.0)
            dp = nt(kv[h, 1, keys, :], grads)
            e_b[i] = e
            d_b[i] = dp
            l_b[...] += jnp.sum(e, axis=0, keepdims=True)
            delta_b[...] += jnp.sum(e * dp, axis=0, keepdims=True)

        for i in reversed(range(BLOCKS)):
            keyed(i, first)
        il = 1.0 / l_b[...]
        delta = delta_b[...] * il

        def second(i, keys):
            p = e_b[i] * il
            ds = (p * (d_b[i] - delta) * score_scale).astype(BF16)
            acc[h, 0, keys, :] += jnp.dot(ds, queries, preferred_element_type=F32)
            acc[h, 1, keys, :] += jnp.dot(p.astype(BF16), grads, preferred_element_type=F32)
            dqt[...] += tn(kv[h, 0, keys, :], ds)

        for i in range(BLOCKS):
            keyed(i, second)
        dq = jnp.transpose(dqt[...])
        dq_raw, gain_part = norm_back(raw, inv, qg[...], dq)
        gain_acc[0:1, :] += gain_part
        dq_raw = dq_raw.astype(BF16)
        dq_s[s, :, 0:D] = dq_raw[0:T]
        dq_s[s, :, D : 2 * D] = dq_raw[T : 2 * T]

        @pl.when(qb == x)
        def _():
            put_local(h, s).start()

        @pl.when(qb != x)
        def _():
            put_remote(h, s).start()

    def dq_place(h):
        return dq_o.at[:, pl.ds(pl.multiple_of(x * 4 * D + h * 2 * D, 2 * D), 2 * D)]

    def put_local(h, s):
        return pltpu.make_async_copy(dq_s.at[s], dq_place(h), o_loc.at[h])

    def put_remote(h, s):
        return remote(dq_s.at[s], dq_place(h), o_snd.at[h], o_rcv.at[h], side)

    def start_two(h):
        @pl.when(has_prev2)
        def _():
            term[h, 0] = acc[h, :, 0 : 2 * T, :].astype(BF16)
            back_two(h).start()

    def start_one(h):
        @pl.when(has_prev & has_next)
        def _():
            back_two(h).wait_recv()
            term[h, 1] = (acc[h, :, 2 * T : 4 * T, :] + got[h, 0].astype(F32)).astype(BF16)

        @pl.when(has_prev & jnp.logical_not(has_next))
        def _():
            term[h, 1] = acc[h, :, 2 * T : 4 * T, :].astype(BF16)

        @pl.when(has_prev)
        def _():
            back_one(h).start()

    def outs(h):
        place = pl.ds(pl.multiple_of(x * 2 * D + h * D, D), D)
        other = pl.ds(pl.multiple_of((1 - x) * T, T), T)
        made = []
        for i, (src, dst) in enumerate(((dk_s, dk_o), (dv_s, dv_o))):
            made.append(pltpu.make_async_copy(src.at[h, mine], dst.at[:, place], p_loc.at[h, i]))
            made.append(remote(src.at[h, other], dst.at[:, place], p_snd.at[h, i], p_rcv.at[h, i], side))
        return made

    def finish(h):
        @pl.when(has_next)
        def _():
            back_one(h).wait_recv()
            acc[h, :, 4 * T : 6 * T, :] += got[h, 1].astype(F32)

        raw = k_b[:, h * D : (h + 1) * D].astype(F32)
        dk_raw, gain_part = norm_back(raw, inverse_norm(raw), kg[...], acc[h, 0, 4 * T : 6 * T, :])
        gain_acc[1:2, :] += gain_part
        dk_s[h] = dk_raw.astype(BF16)
        dv_s[h] = acc[h, 1, 4 * T : 6 * T, :].astype(BF16)
        for copy in outs(h):
            copy.start()

    def step(s, carry):
        @pl.when((s == 0) & has_prev2)
        def _():
            send_on(0).wait_recv()

        @pl.when(s == 1)
        def _():
            forward(1)

        @pl.when((s == 2) & has_prev2)
        def _():
            send_on(1).wait_recv()

        attend(s)

        @pl.when(s == 1)
        def _():
            start_two(0)

        @pl.when(s == 2)
        def _():
            start_one(0)

        return carry

    lax.fori_loop(0, 4, step, 0)
    start_two(1)
    finish(0)
    start_one(1)
    finish(1)

    def spread(size, me, axis, buf, snd, rcv):
        copies = []
        for k in range(1, size):
            copies.append(remote(buf.at[me], buf.at[me], snd.at[k], rcv.at[k], {axis: lax.rem(me + k, size)}))
        for copy in copies:
            copy.start()
        for copy in copies:
            copy.wait_recv()
        return copies

    gain_c[c] = gain_acc[...]
    sent = spread(n, c, "ctx", gain_c, c_snd, c_rcv)
    gain_t[tp] = jnp.sum(gain_c[...], axis=0)
    sent += spread(m, tp, "tp", gain_t, t_snd, t_rcv)
    total = jnp.sum(gain_t[...], axis=0)
    gain_o[0:1, :] = total[0:1] * ((n * T * Q_HEADS) ** -0.5)
    gain_o[1:2, :] = total[1:2] * ((n * T * KV_HEADS) ** -0.5)

    for copy in sent:
        copy.wait_send()
    for far, _ in swaps:
        far.wait_send()
    for h in range(2):
        @pl.when(has_next)
        def _():
            send_own(h).wait_send()

        @pl.when(has_prev & has_next)
        def _():
            send_on(h).wait_send()

        @pl.when(has_prev2)
        def _():
            back_two(h).wait_send()

        @pl.when(has_prev)
        def _():
            back_one(h).wait_send()

        put_local(h, 2 * h + x).wait()
        put_remote(h, 2 * h + 1 - x).wait()
        for copy in outs(h):
            copy.wait()


def per_device(n, m, q_raw, k_raw, v_cur, d_out, q_gain, k_gain):
    dma = pltpu.SemaphoreType.DMA
    anywhere = pl.BlockSpec(memory_space=pl.ANY)
    vmem = pl.BlockSpec(memory_space=pltpu.VMEM)
    dq_raw, dk_raw, dv, gains = pl.pallas_call(
        functools.partial(kernel, n, m),
        out_shape=(
            jax.ShapeDtypeStruct(q_raw.shape, BF16),
            jax.ShapeDtypeStruct(k_raw.shape, BF16),
            jax.ShapeDtypeStruct(v_cur.shape, BF16),
            jax.ShapeDtypeStruct((2, D), F32),
        ),
        in_specs=[anywhere] * 4 + [vmem] * 2,
        out_specs=(anywhere, anywhere, anywhere, vmem),
        scratch_shapes=[
            pltpu.VMEM((2 * T, 4 * D), BF16),
            pltpu.VMEM((2 * T, 4 * D), BF16),
            pltpu.VMEM((2 * T, 2 * D), BF16),
            pltpu.VMEM((2 * T, 2 * D), BF16),
            pltpu.VMEM((2, 2, 6 * T, D), BF16),
            pltpu.VMEM((BLOCKS, T, 2 * T), F32),
            pltpu.VMEM((BLOCKS, T, 2 * T), F32),
            pltpu.VMEM((1, 2 * T), F32),
            pltpu.VMEM((1, 2 * T), F32),
            pltpu.VMEM((D, 2 * T), F32),
            pltpu.VMEM((2, 2, 6 * T, D), F32),
            pltpu.VMEM((2, 2, 2, 2 * T, D), BF16),
            pltpu.VMEM((2, 2, 2, 2 * T, D), BF16),
            pltpu.VMEM((4, T, 2 * D), BF16),
            pltpu.VMEM((2, 2 * T, D), BF16),
            pltpu.VMEM((2, 2 * T, D), BF16),
            pltpu.VMEM((8, D), F32),
            pltpu.VMEM((n, 8, D), F32),
            pltpu.VMEM((m, 8, D), F32),
            dma((4,)), dma((4,)), dma((4,)),
            dma((2, 2)), dma((2, 2)), dma((2, 2)), dma((2, 2)),
            dma((2,)), dma((2,)), dma((2,)),
            dma((2, 2)), dma((2, 2)), dma((2, 2)),
            dma((n,)), dma((n,)), dma((m,)), dma((m,)),
        ],
        compiler_params=pltpu.CompilerParams(
            collective_id=0, has_side_effects=True, vmem_limit_bytes=48 * 1024 * 1024
        ),
    )(q_raw, k_raw, v_cur, d_out, q_gain.reshape(1, D), k_gain.reshape(1, D))
    return (dq_raw, dk_raw, dv, gains[0], gains[1])


def solution(mesh):
    return jax.shard_map(
        functools.partial(per_device, mesh.shape["ctx"], mesh.shape["tp"]),
        mesh=mesh,
        in_specs=(P("ctx", "tp"), P("ctx", "tp"), P("ctx", "tp"), P("ctx", "tp"), P(), P()),
        out_specs=(P("ctx", "tp"), P("ctx", "tp"), P("ctx", "tp"), P(), P()),
        check_vma=False,
    )
```

```python
import functools

import jax
import jax.numpy as jnp
from jax import lax
from jax.experimental import pallas as pl
from jax.experimental.pallas import tpu as pltpu
from jax.sharding import PartitionSpec as P

Q_HEADS = 32
KV_HEADS = 16
HEAD_DIM = 128
WINDOW = 1024

score_scale = 168.0 ** (-0.5)
epsilon = 1e-06
MESH = pl.DeviceIdType.MESH
F32 = jnp.float32
BF16 = jnp.bfloat16
T = 256
D = HEAD_DIM
BLOCKS = 5


def nt(a, b):
    return lax.dot_general(a, b, (((1,), (1,)), ((), ())), preferred_element_type=F32)


def tn(a, b):
    return lax.dot_general(a, b, (((0,), (0,)), ((), ())), preferred_element_type=F32)


def inverse_norm(x):
    return lax.rsqrt(jnp.mean(x * x, axis=-1, keepdims=True) + epsilon)


def norm_back(x, inv, gain, grad):
    unit = x * inv
    pulled = grad * gain
    raw = inv * (pulled - unit * jnp.mean(pulled * unit, axis=-1, keepdims=True))
    return raw, jnp.sum(grad * unit, axis=0, keepdims=True)


def kernel(n, m, q_in, k_in, v_in, g_in, qg, kg, dq_o, dk_o, dv_o, gain_o,
           q_b, g_b, k_b, v_b, kv, e_b, d_b, l_b, delta_b, dqt, acc, term, got, dq_s, dk_s, dv_s,
           gain_acc, gain_c, gain_t,
           x_loc, x_snd, x_rcv, f_snd, f_rcv, b_snd, b_rcv, o_loc, o_snd, o_rcv,
           p_loc, p_snd, p_rcv, c_snd, c_rcv, t_snd, t_rcv):
    c = lax.axis_index("ctx")
    tp = lax.axis_index("tp")
    x = lax.rem(c, 2)
    xp = c + 1 - 2 * x
    up = {"ctx": c + 2}
    down = {"ctx": c - 2}
    side = {"ctx": xp}
    has_next = c + 2 < n
    has_prev = c >= 2
    has_prev2 = c >= 4

    barrier = pltpu.get_barrier_semaphore()
    for k in range(1, n):
        pl.semaphore_signal(barrier, inc=1, device_id={"ctx": lax.rem(c + k, n)}, device_id_type=MESH)
    for k in range(1, m):
        pl.semaphore_signal(barrier, inc=1, device_id={"tp": lax.rem(tp + k, m)}, device_id_type=MESH)
    pl.semaphore_wait(barrier, n - 1 + m - 1)

    def remote(src, dst, snd, rcv, to):
        return pltpu.make_async_remote_copy(src_ref=src, dst_ref=dst, send_sem=snd, recv_sem=rcv,
                                            device_id=to, device_id_type=MESH)

    mine = pl.ds(pl.multiple_of(x * T, T), T)
    theirs = pl.ds(pl.multiple_of((1 - x) * T, T), T)

    def swap(i, src, dst, h, width):
        there = pl.ds(pl.multiple_of((1 - x) * 2 * width + h * width, D), width)
        here = pl.ds(pl.multiple_of(x * 2 * width + h * width, D), width)
        cols = slice(h * width, (h + 1) * width)
        return (remote(src.at[:, there], dst.at[mine, cols], x_snd.at[i, h], x_rcv.at[i, h], side),
                pltpu.make_async_copy(src.at[:, here], dst.at[mine, cols], x_loc.at[i, h]))

    keys_in = [[swap(0, k_in, k_b, h, D), swap(1, v_in, v_b, h, D)] for h in range(2)]
    rows_in = [[swap(2, q_in, q_b, h, 2 * D), swap(3, g_in, g_b, h, 2 * D)] for h in range(2)]
    for h in range(2):
        for far, near in keys_in[h]:
            near.start()
            far.start()

    def half_rows(hop, half):
        return pl.ds(pl.multiple_of((4 - 2 * hop) * T + half * T, T), T)

    def send_own(h, half):
        return remote(kv.at[h, :, half_rows(0, half)], kv.at[h, :, half_rows(1, half)],
                      f_snd.at[h, 0, half], f_rcv.at[h, 0, half], up)

    def send_on(h, half):
        return remote(kv.at[h, :, half_rows(1, half)], kv.at[h, :, half_rows(2, half)],
                      f_snd.at[h, 1, half], f_rcv.at[h, 1, half], up)

    def back_two(h, half):
        return remote(term.at[h, 0, half], got.at[h, 0, half], b_snd.at[h, 0, half], b_rcv.at[h, 0, half], down)

    def back_one(h, half):
        return remote(term.at[h, 1, half], got.at[h, 1, half], b_snd.at[h, 1, half], b_rcv.at[h, 1, half], down)

    def forward(h, half):
        @pl.when(has_prev)
        def _():
            send_own(h, half).wait_recv()

        @pl.when(has_prev & has_next)
        def _():
            send_on(h, half).start()

    def fill(h, half, rows):
        cols = slice(h * D, (h + 1) * D)
        raw = k_b[rows, cols].astype(F32)
        kv[h, 0, half_rows(0, half), :] = (raw * inverse_norm(raw) * kg[...]).astype(BF16)
        kv[h, 1, half_rows(0, half), :] = v_b[rows, cols]

    def start_own(h, half):
        @pl.when(has_next)
        def _():
            send_own(h, half).start()

    for far, near in keys_in[0]:
        near.wait()
    fill(0, x, mine)
    start_own(0, x)
    for far, near in keys_in[1]:
        near.wait()
    fill(1, x, mine)
    gain_acc[...] = jnp.zeros_like(gain_acc)
    for far, near in keys_in[0]:
        far.wait_recv()
    fill(0, 1 - x, theirs)
    start_own(0, 1 - x)
    for far, near in keys_in[1]:
        far.wait_recv()
    for h in range(2):
        for far, near in rows_in[h]:
            near.start()
            far.start()
    fill(1, 1 - x, theirs)
    forward(0, x)
    forward(0, 1 - x)
    start_own(1, x)
    start_own(1, 1 - x)
    acc[...] = jnp.zeros_like(acc)

    row = lax.broadcasted_iota(jnp.int32, (T, 2 * T), 0)
    col = lax.rem(lax.broadcasted_iota(jnp.int32, (T, 2 * T), 1), T)

    def attend(s):
        h = s // 2
        qb = lax.rem(s, 2)
        rows = pl.ds(pl.multiple_of(qb * T, T), T)
        col0 = pl.ds(pl.multiple_of(h * 2 * D, D), D)
        col1 = pl.ds(pl.multiple_of(h * 2 * D + D, D), D)
        raw = jnp.concatenate([q_b[rows, col0], q_b[rows, col1]], axis=0).astype(F32)
        grads = jnp.concatenate([g_b[rows, col0], g_b[rows, col1]], axis=0)
        inv = inverse_norm(raw)
        queries = (raw * inv * qg[...]).astype(BF16)
        l_b[...] = jnp.zeros_like(l_b)
        delta_b[...] = jnp.zeros_like(delta_b)
        dqt[...] = jnp.zeros_like(dqt)

        def keyed(i, body):
            start = pl.multiple_of((qb + i) * T, T)
            if i == BLOCKS - 1:
                body(i, pl.ds(start, T))
            else:
                @pl.when(c - x - 4 + qb + i >= 0)
                def _():
                    body(i, pl.ds(start, T))

        def first(i, keys):
            scores = nt(kv[h, 0, keys, :], queries)
            e = jnp.exp(scores * score_scale)
            if i == 0:
                e = jnp.where(col < row, e, 0.0)
            if i == BLOCKS - 1:
                e = jnp.where(col >= row, e, 0.0)
            dp = nt(kv[h, 1, keys, :], grads)
            e_b[i] = e
            d_b[i] = dp
            l_b[...] += jnp.sum(e, axis=0, keepdims=True)
            delta_b[...] += jnp.sum(e * dp, axis=0, keepdims=True)

        for i in reversed(range(BLOCKS)):
            keyed(i, first)
        il = 1.0 / l_b[...]
        delta = delta_b[...] * il

        def second(i, keys):
            p = e_b[i] * il
            ds = (p * (d_b[i] - delta) * score_scale).astype(BF16)
            acc[h, 0, keys, :] += jnp.dot(ds, queries, preferred_element_type=F32)
            acc[h, 1, keys, :] += jnp.dot(p.astype(BF16), grads, preferred_element_type=F32)
            dqt[...] += tn(kv[h, 0, keys, :], ds)

        for i in range(BLOCKS):
            keyed(i, second)
        dq = jnp.transpose(dqt[...])
        dq_raw, gain_part = norm_back(raw, inv, qg[...], dq)
        gain_acc[0:1, :] += gain_part
        dq_raw = dq_raw.astype(BF16)
        dq_s[s, :, 0:D] = dq_raw[0:T]
        dq_s[s, :, D : 2 * D] = dq_raw[T : 2 * T]

        @pl.when(qb == x)
        def _():
            put_local(h, s).start()

        @pl.when(qb != x)
        def _():
            put_remote(h, s).start()

    def dq_place(h):
        return dq_o.at[:, pl.ds(pl.multiple_of(x * 4 * D + h * 2 * D, 2 * D), 2 * D)]

    def put_local(h, s):
        return pltpu.make_async_copy(dq_s.at[s], dq_place(h), o_loc.at[h])

    def put_remote(h, s):
        return remote(dq_s.at[s], dq_place(h), o_snd.at[h], o_rcv.at[h], side)

    def start_two(h, half):
        @pl.when(has_prev2)
        def _():
            term[h, 0, half] = acc[h, :, half_rows(2, half), :].astype(BF16)
            back_two(h, half).start()

    def start_one(h, half):
        @pl.when(has_prev & has_next)
        def _():
            back_two(h, half).wait_recv()
            term[h, 1, half] = (acc[h, :, half_rows(1, half), :] + got[h, 0, half].astype(F32)).astype(BF16)

        @pl.when(has_prev & jnp.logical_not(has_next))
        def _():
            term[h, 1, half] = acc[h, :, half_rows(1, half), :].astype(BF16)

        @pl.when(has_prev)
        def _():
            back_one(h, half).start()

    def place(dst, h):
        return dst.at[:, pl.ds(pl.multiple_of(x * 2 * D + h * D, D), D)]

    def keep(h):
        return [pltpu.make_async_copy(src.at[h, mine], place(dst, h), p_loc.at[h, i])
                for i, (src, dst) in enumerate(((dk_s, dk_o), (dv_s, dv_o)))]

    def give(h):
        return [remote(src.at[h, theirs], place(dst, h), p_snd.at[h, i], p_rcv.at[h, i], side)
                for i, (src, dst) in enumerate(((dk_s, dk_o), (dv_s, dv_o)))]

    def finish(h, half):
        rows = pl.ds(pl.multiple_of(half * T, T), T)
        here = half_rows(0, half)

        @pl.when(has_next)
        def _():
            back_one(h, half).wait_recv()
            acc[h, :, here, :] += got[h, 1, half].astype(F32)

        raw = k_b[rows, h * D : (h + 1) * D].astype(F32)
        dk_raw, gain_part = norm_back(raw, inverse_norm(raw), kg[...], acc[h, 0, here, :])
        gain_acc[1:2, :] += gain_part
        dk_s[h, rows] = dk_raw.astype(BF16)
        dv_s[h, rows] = acc[h, 1, here, :].astype(BF16)

        @pl.when(x == half)
        def _():
            for copy in keep(h):
                copy.start()

        @pl.when(x != half)
        def _():
            for copy in give(h):
                copy.start()

    def arrived(h):
        @pl.when(has_prev2)
        def _():
            send_on(h, 0).wait_recv()
            send_on(h, 1).wait_recv()

        for far, near in rows_in[h]:
            near.wait()
            far.wait_recv()

    def step(s, carry):
        @pl.when(s == 0)
        def _():
            arrived(0)

        @pl.when(s == 1)
        def _():
            forward(1, x)
            forward(1, 1 - x)

        @pl.when(s == 2)
        def _():
            arrived(1)

        attend(s)

        @pl.when(s == 0)
        def _():
            start_two(0, 0)

        @pl.when(s == 1)
        def _():
            start_two(0, 1)
            start_one(0, 0)

        @pl.when(s == 2)
        def _():
            start_one(0, 1)
            start_two(1, 0)

        return carry

    lax.fori_loop(0, 4, step, 0)
    start_two(1, 1)
    start_one(1, 0)
    finish(0, 0)
    finish(0, 1)
    start_one(1, 1)
    finish(1, 0)
    finish(1, 1)

    def spread(size, me, axis, buf, snd, rcv):
        copies = []
        for k in range(1, size):
            copies.append(remote(buf.at[me], buf.at[me], snd.at[k], rcv.at[k], {axis: lax.rem(me + k, size)}))
        for copy in copies:
            copy.start()
        for copy in copies:
            copy.wait_recv()
        return copies

    gain_c[c] = gain_acc[...]
    sent = spread(n, c, "ctx", gain_c, c_snd, c_rcv)
    gain_t[tp] = jnp.sum(gain_c[...], axis=0)
    sent += spread(m, tp, "tp", gain_t, t_snd, t_rcv)
    total = jnp.sum(gain_t[...], axis=0)
    gain_o[0:1, :] = total[0:1] * ((n * T * Q_HEADS) ** -0.5)
    gain_o[1:2, :] = total[1:2] * ((n * T * KV_HEADS) ** -0.5)

    for copy in sent:
        copy.wait_send()
    for h in range(2):
        for far, _ in keys_in[h] + rows_in[h]:
            far.wait_send()
        for half in range(2):
            @pl.when(has_next)
            def _():
                send_own(h, half).wait_send()

            @pl.when(has_prev & has_next)
            def _():
                send_on(h, half).wait_send()

            @pl.when(has_prev2)
            def _():
                back_two(h, half).wait_send()

            @pl.when(has_prev)
            def _():
                back_one(h, half).wait_send()

        put_local(h, 2 * h + x).wait()
        put_remote(h, 2 * h + 1 - x).wait()
        for copy in keep(h) + give(h):
            copy.wait()


def per_device(n, m, q_raw, k_raw, v_cur, d_out, q_gain, k_gain):
    dma = pltpu.SemaphoreType.DMA
    anywhere = pl.BlockSpec(memory_space=pl.ANY)
    vmem = pl.BlockSpec(memory_space=pltpu.VMEM)
    dq_raw, dk_raw, dv, gains = pl.pallas_call(
        functools.partial(kernel, n, m),
        out_shape=(
            jax.ShapeDtypeStruct(q_raw.shape, BF16),
            jax.ShapeDtypeStruct(k_raw.shape, BF16),
            jax.ShapeDtypeStruct(v_cur.shape, BF16),
            jax.ShapeDtypeStruct((2, D), F32),
        ),
        in_specs=[pl.BlockSpec(memory_space=pltpu.HBM)] * 4 + [vmem] * 2,
        out_specs=(anywhere, anywhere, anywhere, vmem),
        scratch_shapes=[
            pltpu.VMEM((2 * T, 4 * D), BF16),
            pltpu.VMEM((2 * T, 4 * D), BF16),
            pltpu.VMEM((2 * T, 2 * D), BF16),
            pltpu.VMEM((2 * T, 2 * D), BF16),
            pltpu.VMEM((2, 2, 6 * T, D), BF16),
            pltpu.VMEM((BLOCKS, T, 2 * T), F32),
            pltpu.VMEM((BLOCKS, T, 2 * T), F32),
            pltpu.VMEM((1, 2 * T), F32),
            pltpu.VMEM((1, 2 * T), F32),
            pltpu.VMEM((D, 2 * T), F32),
            pltpu.VMEM((2, 2, 6 * T, D), F32),
            pltpu.VMEM((2, 2, 2, 2, T, D), BF16),
            pltpu.VMEM((2, 2, 2, 2, T, D), BF16),
            pltpu.VMEM((4, T, 2 * D), BF16),
            pltpu.VMEM((2, 2 * T, D), BF16),
            pltpu.VMEM((2, 2 * T, D), BF16),
            pltpu.VMEM((8, D), F32),
            pltpu.VMEM((n, 8, D), F32),
            pltpu.VMEM((m, 8, D), F32),
            dma((4, 2)), dma((4, 2)), dma((4, 2)),
            dma((2, 2, 2)), dma((2, 2, 2)), dma((2, 2, 2)), dma((2, 2, 2)),
            dma((2,)), dma((2,)), dma((2,)),
            dma((2, 2)), dma((2, 2)), dma((2, 2)),
            dma((n,)), dma((n,)), dma((m,)), dma((m,)),
        ],
        compiler_params=pltpu.CompilerParams(
            collective_id=0, has_side_effects=True, vmem_limit_bytes=48 * 1024 * 1024
        ),
    )(q_raw, k_raw, v_cur, d_out, q_gain.reshape(1, D), k_gain.reshape(1, D))
    return (dq_raw, dk_raw, dv, gains[0], gains[1])


def solution(mesh):
    return jax.shard_map(
        functools.partial(per_device, mesh.shape["ctx"], mesh.shape["tp"]),
        mesh=mesh,
        in_specs=(P("ctx", "tp"), P("ctx", "tp"), P("ctx", "tp"), P("ctx", "tp"), P(), P()),
        out_specs=(P("ctx", "tp"), P("ctx", "tp"), P("ctx", "tp"), P(), P()),
        check_vma=False,
    )
```

```python
import functools

import jax
import jax.numpy as jnp
from jax import lax
from jax.experimental import pallas as pl
from jax.experimental.pallas import tpu as pltpu
from jax.sharding import PartitionSpec as P

Q_HEADS = 32
KV_HEADS = 16
HEAD_DIM = 128
WINDOW = 1024

score_scale = 168.0 ** (-0.5)
epsilon = 1e-06
MESH = pl.DeviceIdType.MESH
F32 = jnp.float32
BF16 = jnp.bfloat16
T = 256
D = HEAD_DIM
BLOCKS = 5


def nt(a, b):
    return lax.dot_general(a, b, (((1,), (1,)), ((), ())), preferred_element_type=F32)


def tn(a, b):
    return lax.dot_general(a, b, (((0,), (0,)), ((), ())), preferred_element_type=F32)


def inverse_norm(x):
    return lax.rsqrt(jnp.mean(x * x, axis=-1, keepdims=True) + epsilon)


def norm_back(x, inv, gain, grad):
    unit = x * inv
    pulled = grad * gain
    raw = inv * (pulled - unit * jnp.mean(pulled * unit, axis=-1, keepdims=True))
    return raw, jnp.sum(grad * unit, axis=0, keepdims=True)


def kernel(n, m, q_in, k_in, v_in, g_in, qg, kg, dq_o, dk_o, dv_o, gain_o,
           q_b, g_b, k_b, v_b, kv, e_b, d_b, l_b, delta_b, dqt, acc, term, got, dq_s, dk_s, dv_s,
           gain_acc, gain_c, gain_t,
           x_loc, x_snd, x_rcv, f_snd, f_rcv, b_snd, b_rcv, o_loc, o_snd, o_rcv,
           p_loc, p_snd, p_rcv, c_snd, c_rcv, t_snd, t_rcv):
    c = lax.axis_index("ctx")
    tp = lax.axis_index("tp")
    x = lax.rem(c, 2)
    xp = c + 1 - 2 * x
    up = {"ctx": c + 2}
    down = {"ctx": c - 2}
    side = {"ctx": xp}
    has_next = c + 2 < n
    has_prev = c >= 2
    has_prev2 = c >= 4

    barrier = pltpu.get_barrier_semaphore()
    for k in range(1, n):
        pl.semaphore_signal(barrier, inc=1, device_id={"ctx": lax.rem(c + k, n)}, device_id_type=MESH)
    for k in range(1, m):
        pl.semaphore_signal(barrier, inc=1, device_id={"tp": lax.rem(tp + k, m)}, device_id_type=MESH)
    pl.semaphore_wait(barrier, n - 1 + m - 1)

    def remote(src, dst, snd, rcv, to):
        return pltpu.make_async_remote_copy(src_ref=src, dst_ref=dst, send_sem=snd, recv_sem=rcv,
                                            device_id=to, device_id_type=MESH)

    mine = pl.ds(pl.multiple_of(x * T, T), T)
    theirs = pl.ds(pl.multiple_of((1 - x) * T, T), T)

    def swap(i, src, dst, h, width):
        there = pl.ds(pl.multiple_of((1 - x) * 2 * width + h * width, D), width)
        here = pl.ds(pl.multiple_of(x * 2 * width + h * width, D), width)
        cols = slice(h * width, (h + 1) * width)
        return (remote(src.at[:, there], dst.at[mine, cols], x_snd.at[i, h], x_rcv.at[i, h], side),
                pltpu.make_async_copy(src.at[:, here], dst.at[mine, cols], x_loc.at[i, h]))

    keys_in = [[swap(0, k_in, k_b, h, D), swap(1, v_in, v_b, h, D)] for h in range(2)]
    rows_in = [[swap(2, q_in, q_b, h, 2 * D), swap(3, g_in, g_b, h, 2 * D)] for h in range(2)]
    for h in range(2):
        for far, near in keys_in[h]:
            near.start()
            far.start()

    def half_rows(hop, half):
        return pl.ds(pl.multiple_of((4 - 2 * hop) * T + half * T, T), T)

    def send_own(h, half):
        return remote(kv.at[h, :, half_rows(0, half)], kv.at[h, :, half_rows(1, half)],
                      f_snd.at[h, 0, half], f_rcv.at[h, 0, half], up)

    def send_on(h, half):
        return remote(kv.at[h, :, half_rows(1, half)], kv.at[h, :, half_rows(2, half)],
                      f_snd.at[h, 1, half], f_rcv.at[h, 1, half], up)

    def back_two(h, half):
        return remote(term.at[h, 0, half], got.at[h, 0, half], b_snd.at[h, 0, half], b_rcv.at[h, 0, half], down)

    def back_one(h, half):
        return remote(term.at[h, 1, half], got.at[h, 1, half], b_snd.at[h, 1, half], b_rcv.at[h, 1, half], down)

    def forward(h, half):
        @pl.when(has_prev)
        def _():
            send_own(h, half).wait_recv()

        @pl.when(has_prev & has_next)
        def _():
            send_on(h, half).start()

    def fill(h, half, rows):
        cols = slice(h * D, (h + 1) * D)
        raw = k_b[rows, cols].astype(F32)
        kv[h, 0, half_rows(0, half), :] = (raw * inverse_norm(raw) * kg[...]).astype(BF16)
        kv[h, 1, half_rows(0, half), :] = v_b[rows, cols]

    def start_own(h, half):
        @pl.when(has_next)
        def _():
            send_own(h, half).start()

    for far, near in keys_in[0]:
        near.wait()
    fill(0, x, mine)
    start_own(0, x)
    for far, near in keys_in[1]:
        near.wait()
    fill(1, x, mine)
    start_own(1, x)
    gain_acc[...] = jnp.zeros_like(gain_acc)
    for far, near in keys_in[0]:
        far.wait_recv()
    fill(0, 1 - x, theirs)
    start_own(0, 1 - x)
    for far, near in keys_in[1]:
        far.wait_recv()
    for h in range(2):
        for far, near in rows_in[h]:
            near.start()
            far.start()
    fill(1, 1 - x, theirs)
    forward(0, x)
    forward(0, 1 - x)
    start_own(1, 1 - x)
    acc[...] = jnp.zeros_like(acc)

    row = lax.broadcasted_iota(jnp.int32, (T, 2 * T), 0)
    col = lax.rem(lax.broadcasted_iota(jnp.int32, (T, 2 * T), 1), T)

    def attend(s):
        h = s // 2
        qb = lax.rem(s, 2)
        rows = pl.ds(pl.multiple_of(qb * T, T), T)
        col0 = pl.ds(pl.multiple_of(h * 2 * D, D), D)
        col1 = pl.ds(pl.multiple_of(h * 2 * D + D, D), D)
        raw = jnp.concatenate([q_b[rows, col0], q_b[rows, col1]], axis=0).astype(F32)
        grads = jnp.concatenate([g_b[rows, col0], g_b[rows, col1]], axis=0)
        inv = inverse_norm(raw)
        queries = (raw * inv * qg[...]).astype(BF16)
        l_b[...] = jnp.zeros_like(l_b)
        delta_b[...] = jnp.zeros_like(delta_b)
        dqt[...] = jnp.zeros_like(dqt)

        def keyed(i, body):
            start = pl.multiple_of((qb + i) * T, T)
            if i == BLOCKS - 1:
                body(i, pl.ds(start, T))
            else:
                @pl.when(c - x - 4 + qb + i >= 0)
                def _():
                    body(i, pl.ds(start, T))

        def first(i, keys):
            scores = nt(kv[h, 0, keys, :], queries)
            e = jnp.exp(scores * score_scale)
            if i == 0:
                e = jnp.where(col < row, e, 0.0)
            if i == BLOCKS - 1:
                e = jnp.where(col >= row, e, 0.0)
            dp = nt(kv[h, 1, keys, :], grads)
            e_b[i] = e
            d_b[i] = dp
            l_b[...] += jnp.sum(e, axis=0, keepdims=True)
            delta_b[...] += jnp.sum(e * dp, axis=0, keepdims=True)

        for i in reversed(range(BLOCKS)):
            if i == 1:
                for g in range(2):
                    @pl.when((s == 2 * g) & has_prev2)
                    def _():
                        send_on(g, 0).wait_recv()
                        send_on(g, 1).wait_recv()

            keyed(i, first)
        il = 1.0 / l_b[...]
        delta = delta_b[...] * il

        def second(i, keys):
            p = e_b[i] * il
            ds = (p * (d_b[i] - delta) * score_scale).astype(BF16)
            acc[h, 0, keys, :] += jnp.dot(ds, queries, preferred_element_type=F32)
            acc[h, 1, keys, :] += jnp.dot(p.astype(BF16), grads, preferred_element_type=F32)
            dqt[...] += tn(kv[h, 0, keys, :], ds)

        for i in range(BLOCKS):
            keyed(i, second)
        dq = jnp.transpose(dqt[...])
        dq_raw, gain_part = norm_back(raw, inv, qg[...], dq)
        gain_acc[0:1, :] += gain_part
        dq_raw = dq_raw.astype(BF16)
        dq_s[s, :, 0:D] = dq_raw[0:T]
        dq_s[s, :, D : 2 * D] = dq_raw[T : 2 * T]

        @pl.when(qb == x)
        def _():
            put_local(h, s).start()

        @pl.when(qb != x)
        def _():
            put_remote(h, s).start()

    def dq_place(h):
        return dq_o.at[:, pl.ds(pl.multiple_of(x * 4 * D + h * 2 * D, 2 * D), 2 * D)]

    def put_local(h, s):
        return pltpu.make_async_copy(dq_s.at[s], dq_place(h), o_loc.at[h])

    def put_remote(h, s):
        return remote(dq_s.at[s], dq_place(h), o_snd.at[h], o_rcv.at[h], side)

    def start_two(h, half):
        @pl.when(has_prev2)
        def _():
            term[h, 0, half] = acc[h, :, half_rows(2, half), :].astype(BF16)
            back_two(h, half).start()

    def start_one(h, half):
        @pl.when(has_prev & has_next)
        def _():
            back_two(h, half).wait_recv()
            term[h, 1, half] = (acc[h, :, half_rows(1, half), :] + got[h, 0, half].astype(F32)).astype(BF16)

        @pl.when(has_prev & jnp.logical_not(has_next))
        def _():
            term[h, 1, half] = acc[h, :, half_rows(1, half), :].astype(BF16)

        @pl.when(has_prev)
        def _():
            back_one(h, half).start()

    def place(dst, h):
        return dst.at[:, pl.ds(pl.multiple_of(x * 2 * D + h * D, D), D)]

    def keep(h):
        return [pltpu.make_async_copy(src.at[h, mine], place(dst, h), p_loc.at[h, i])
                for i, (src, dst) in enumerate(((dk_s, dk_o), (dv_s, dv_o)))]

    def give(h):
        return [remote(src.at[h, theirs], place(dst, h), p_snd.at[h, i], p_rcv.at[h, i], side)
                for i, (src, dst) in enumerate(((dk_s, dk_o), (dv_s, dv_o)))]

    def finish(h, half):
        rows = pl.ds(pl.multiple_of(half * T, T), T)
        here = half_rows(0, half)

        @pl.when(has_next)
        def _():
            back_one(h, half).wait_recv()
            acc[h, :, here, :] += got[h, 1, half].astype(F32)

        raw = k_b[rows, h * D : (h + 1) * D].astype(F32)
        dk_raw, _ = norm_back(raw, inverse_norm(raw), kg[...], acc[h, 0, here, :])
        dk_s[h, rows] = dk_raw.astype(BF16)
        dv_s[h, rows] = acc[h, 1, here, :].astype(BF16)

        @pl.when(x == half)
        def _():
            for copy in keep(h):
                copy.start()

        @pl.when(x != half)
        def _():
            for copy in give(h):
                copy.start()

    def arrived(h):
        for far, near in rows_in[h]:
            near.wait()
            far.wait_recv()

    def step(s, carry):
        @pl.when(s == 0)
        def _():
            arrived(0)

        @pl.when(s == 1)
        def _():
            forward(1, x)
            forward(1, 1 - x)

        @pl.when(s == 2)
        def _():
            arrived(1)

        attend(s)

        @pl.when(s == 0)
        def _():
            start_two(0, 0)

        @pl.when(s == 1)
        def _():
            start_two(0, 1)
            start_one(0, 0)

        @pl.when(s == 2)
        def _():
            start_one(0, 1)
            start_two(1, 0)

        return carry

    lax.fori_loop(0, 4, step, 0)
    start_two(1, 1)
    start_one(1, 0)

    def key_gain(hop):
        rows = slice((4 - 2 * hop) * T, (6 - 2 * hop) * T)
        for h in range(2):
            gain_acc[1:2, :] += jnp.sum(acc[h, 0, rows, :] * kv[h, 0, rows, :].astype(F32), axis=0, keepdims=True)

    key_gain(0)
    pl.when(has_prev)(lambda: key_gain(1))
    pl.when(has_prev2)(lambda: key_gain(2))

    def spread(size, me, axis, buf, snd, rcv):
        copies = []
        for k in range(1, size):
            copies.append(remote(buf.at[me], buf.at[me], snd.at[k], rcv.at[k], {axis: lax.rem(me + k, size)}))
        for copy in copies:
            copy.start()
        return copies

    gain_c[c] = gain_acc[...]
    over_ctx = spread(n, c, "ctx", gain_c, c_snd, c_rcv)
    finish(0, 0)
    finish(0, 1)
    start_one(1, 1)
    for copy in over_ctx:
        copy.wait_recv()
    gain_t[tp] = jnp.sum(gain_c[...], axis=0)
    over_tp = spread(m, tp, "tp", gain_t, t_snd, t_rcv)
    finish(1, 0)
    finish(1, 1)
    for copy in over_tp:
        copy.wait_recv()
    total = jnp.sum(gain_t[...], axis=0)
    gain_o[0:1, :] = total[0:1] * ((n * T * Q_HEADS) ** -0.5)
    gain_o[1:2, :] = total[1:2] / kg[...] * ((n * T * KV_HEADS) ** -0.5)

    for copy in over_ctx + over_tp:
        copy.wait_send()
    for h in range(2):
        for far, _ in keys_in[h] + rows_in[h]:
            far.wait_send()
        for half in range(2):
            @pl.when(has_next)
            def _():
                send_own(h, half).wait_send()

            @pl.when(has_prev & has_next)
            def _():
                send_on(h, half).wait_send()

            @pl.when(has_prev2)
            def _():
                back_two(h, half).wait_send()

            @pl.when(has_prev)
            def _():
                back_one(h, half).wait_send()

        put_local(h, 2 * h + x).wait()
        put_remote(h, 2 * h + 1 - x).wait()
        for copy in keep(h) + give(h):
            copy.wait()


def per_device(n, m, q_raw, k_raw, v_cur, d_out, q_gain, k_gain):
    dma = pltpu.SemaphoreType.DMA
    anywhere = pl.BlockSpec(memory_space=pl.ANY)
    vmem = pl.BlockSpec(memory_space=pltpu.VMEM)
    dq_raw, dk_raw, dv, gains = pl.pallas_call(
        functools.partial(kernel, n, m),
        out_shape=(
            jax.ShapeDtypeStruct(q_raw.shape, BF16),
            jax.ShapeDtypeStruct(k_raw.shape, BF16),
            jax.ShapeDtypeStruct(v_cur.shape, BF16),
            jax.ShapeDtypeStruct((2, D), F32),
        ),
        in_specs=[pl.BlockSpec(memory_space=pltpu.HBM)] * 4 + [vmem] * 2,
        out_specs=(anywhere, anywhere, anywhere, vmem),
        scratch_shapes=[
            pltpu.VMEM((2 * T, 4 * D), BF16),
            pltpu.VMEM((2 * T, 4 * D), BF16),
            pltpu.VMEM((2 * T, 2 * D), BF16),
            pltpu.VMEM((2 * T, 2 * D), BF16),
            pltpu.VMEM((2, 2, 6 * T, D), BF16),
            pltpu.VMEM((BLOCKS, T, 2 * T), F32),
            pltpu.VMEM((BLOCKS, T, 2 * T), F32),
            pltpu.VMEM((1, 2 * T), F32),
            pltpu.VMEM((1, 2 * T), F32),
            pltpu.VMEM((D, 2 * T), F32),
            pltpu.VMEM((2, 2, 6 * T, D), F32),
            pltpu.VMEM((2, 2, 2, 2, T, D), BF16),
            pltpu.VMEM((2, 2, 2, 2, T, D), BF16),
            pltpu.VMEM((4, T, 2 * D), BF16),
            pltpu.VMEM((2, 2 * T, D), BF16),
            pltpu.VMEM((2, 2 * T, D), BF16),
            pltpu.VMEM((8, D), F32),
            pltpu.VMEM((n, 8, D), F32),
            pltpu.VMEM((m, 8, D), F32),
            dma((4, 2)), dma((4, 2)), dma((4, 2)),
            dma((2, 2, 2)), dma((2, 2, 2)), dma((2, 2, 2)), dma((2, 2, 2)),
            dma((2,)), dma((2,)), dma((2,)),
            dma((2, 2)), dma((2, 2)), dma((2, 2)),
            dma((n,)), dma((n,)), dma((m,)), dma((m,)),
        ],
        compiler_params=pltpu.CompilerParams(
            collective_id=0, has_side_effects=True, vmem_limit_bytes=63 * 1024 * 1024
        ),
    )(q_raw, k_raw, v_cur, d_out, q_gain.reshape(1, D), k_gain.reshape(1, D))
    return (dq_raw, dk_raw, dv, gains[0], gains[1])


def solution(mesh):
    return jax.shard_map(
        functools.partial(per_device, mesh.shape["ctx"], mesh.shape["tp"]),
        mesh=mesh,
        in_specs=(P("ctx", "tp"), P("ctx", "tp"), P("ctx", "tp"), P("ctx", "tp"), P(), P()),
        out_specs=(P("ctx", "tp"), P("ctx", "tp"), P("ctx", "tp"), P(), P()),
        check_vma=False,
    )
```

```python
import functools

import jax
import jax.numpy as jnp
from jax import lax
from jax.experimental import pallas as pl
from jax.experimental.pallas import tpu as pltpu
from jax.sharding import PartitionSpec as P

Q_HEADS = 32
KV_HEADS = 16
HEAD_DIM = 128
WINDOW = 1024

score_scale = 168.0 ** (-0.5)
epsilon = 1e-06
MESH = pl.DeviceIdType.MESH
F32 = jnp.float32
BF16 = jnp.bfloat16
T = 256
D = HEAD_DIM
BLOCKS = 5


def nt(a, b):
    return lax.dot_general(a, b, (((1,), (1,)), ((), ())), preferred_element_type=F32)


def tn(a, b):
    return lax.dot_general(a, b, (((0,), (0,)), ((), ())), preferred_element_type=F32)


def inverse_norm(x):
    return lax.rsqrt(jnp.mean(x * x, axis=-1, keepdims=True) + epsilon)


def norm_back(x, inv, gain, grad):
    unit = x * inv
    pulled = grad * gain
    raw = inv * (pulled - unit * jnp.mean(pulled * unit, axis=-1, keepdims=True))
    return raw, jnp.sum(grad * unit, axis=0, keepdims=True)


def kernel(n, m, q_in, k_in, v_in, g_in, qg, kg, dq_o, dk_o, dv_o, gain_o,
           q_b, g_b, k_b, v_b, kv, e_b, d_b, l_b, delta_b, dqt, acc, term, got, dq_s, dk_s, dv_s,
           gain_acc, gain_c, gain_t,
           x_loc, x_snd, x_rcv, f_snd, f_rcv, b_snd, b_rcv, o_loc, o_snd, o_rcv,
           p_loc, p_snd, p_rcv, c_snd, c_rcv, t_snd, t_rcv):
    c = lax.axis_index("ctx")
    tp = lax.axis_index("tp")
    x = lax.rem(c, 2)
    xp = c + 1 - 2 * x
    up = {"ctx": c + 2}
    down = {"ctx": c - 2}
    side = {"ctx": xp}
    has_next = c + 2 < n
    has_prev = c >= 2
    has_prev2 = c >= 4

    barrier = pltpu.get_barrier_semaphore()
    for k in range(1, n):
        pl.semaphore_signal(barrier, inc=1, device_id={"ctx": lax.rem(c + k, n)}, device_id_type=MESH)
    for k in range(1, m):
        pl.semaphore_signal(barrier, inc=1, device_id={"tp": lax.rem(tp + k, m)}, device_id_type=MESH)
    pl.semaphore_wait(barrier, n - 1 + m - 1)

    def remote(src, dst, snd, rcv, to):
        return pltpu.make_async_remote_copy(src_ref=src, dst_ref=dst, send_sem=snd, recv_sem=rcv,
                                            device_id=to, device_id_type=MESH)

    mine = pl.ds(pl.multiple_of(x * T, T), T)
    theirs = pl.ds(pl.multiple_of((1 - x) * T, T), T)

    def swap(i, src, dst, h, width):
        there = pl.ds(pl.multiple_of((1 - x) * 2 * width + h * width, D), width)
        here = pl.ds(pl.multiple_of(x * 2 * width + h * width, D), width)
        cols = slice(h * width, (h + 1) * width)
        return (remote(src.at[:, there], dst.at[mine, cols], x_snd.at[i, h], x_rcv.at[i, h], side),
                pltpu.make_async_copy(src.at[:, here], dst.at[mine, cols], x_loc.at[i, h]))

    keys_in = [[swap(0, k_in, k_b, h, D), swap(1, v_in, v_b, h, D)] for h in range(2)]
    rows_in = [[swap(2, q_in, q_b, h, 2 * D), swap(3, g_in, g_b, h, 2 * D)] for h in range(2)]
    for h in range(2):
        for far, near in keys_in[h]:
            near.start()
            far.start()

    def half_rows(hop, half):
        return pl.ds(pl.multiple_of((4 - 2 * hop) * T + half * T, T), T)

    def send_own(h, half):
        return remote(kv.at[h, :, half_rows(0, half)], kv.at[h, :, half_rows(1, half)],
                      f_snd.at[h, 0, half], f_rcv.at[h, 0, half], up)

    def send_on(h, half):
        return remote(kv.at[h, :, half_rows(1, half)], kv.at[h, :, half_rows(2, half)],
                      f_snd.at[h, 1, half], f_rcv.at[h, 1, half], up)

    def back_two(h, half):
        return remote(term.at[h, 0, half], got.at[h, 0, half], b_snd.at[h, 0, half], b_rcv.at[h, 0, half], down)

    def back_one(h, half):
        return remote(term.at[h, 1, half], got.at[h, 1, half], b_snd.at[h, 1, half], b_rcv.at[h, 1, half], down)

    def forward(h, half):
        @pl.when(has_prev)
        def _():
            send_own(h, half).wait_recv()

        @pl.when(has_prev & has_next)
        def _():
            send_on(h, half).start()

    def fill(h, half, rows):
        cols = slice(h * D, (h + 1) * D)
        raw = k_b[rows, cols].astype(F32)
        kv[h, 0, half_rows(0, half), :] = (raw * inverse_norm(raw) * kg[...]).astype(BF16)
        kv[h, 1, half_rows(0, half), :] = v_b[rows, cols]

    def start_own(h, half):
        @pl.when(has_next)
        def _():
            send_own(h, half).start()

    for far, near in keys_in[0]:
        near.wait()
    fill(0, x, mine)
    start_own(0, x)
    for far, near in keys_in[1]:
        near.wait()
    fill(1, x, mine)
    start_own(1, x)
    gain_acc[...] = jnp.zeros_like(gain_acc)
    for far, near in keys_in[0]:
        far.wait_recv()
    fill(0, 1 - x, theirs)
    start_own(0, 1 - x)
    for far, near in keys_in[1]:
        far.wait_recv()
    for far, near in rows_in[0]:
        near.start()
        far.start()
    fill(1, 1 - x, theirs)
    forward(0, x)
    forward(0, 1 - x)
    for far, near in rows_in[1]:
        near.start()
        far.start()
    start_own(1, 1 - x)
    acc[...] = jnp.zeros_like(acc)

    row = lax.broadcasted_iota(jnp.int32, (T, 2 * T), 0)
    col = lax.rem(lax.broadcasted_iota(jnp.int32, (T, 2 * T), 1), T)

    def attend(s):
        h = s // 2
        qb = lax.rem(s, 2)
        rows = pl.ds(pl.multiple_of(qb * T, T), T)
        col0 = pl.ds(pl.multiple_of(h * 2 * D, D), D)
        col1 = pl.ds(pl.multiple_of(h * 2 * D + D, D), D)
        raw = jnp.concatenate([q_b[rows, col0], q_b[rows, col1]], axis=0).astype(F32)
        grads = jnp.concatenate([g_b[rows, col0], g_b[rows, col1]], axis=0)
        inv = inverse_norm(raw)
        queries = (raw * inv * qg[...]).astype(BF16)
        l_b[...] = jnp.zeros_like(l_b)
        delta_b[...] = jnp.zeros_like(delta_b)
        dqt[...] = jnp.zeros_like(dqt)

        def keyed(i, body):
            start = pl.multiple_of((qb + i) * T, T)
            if i == BLOCKS - 1:
                body(i, pl.ds(start, T))
            else:
                @pl.when(c - x - 4 + qb + i >= 0)
                def _():
                    body(i, pl.ds(start, T))

        def each(which, body):
            @pl.when(has_prev2)
            def _():
                for i in which:
                    body(i, pl.ds(pl.multiple_of((qb + i) * T, T), T))

            @pl.when(jnp.logical_not(has_prev2))
            def _():
                for i in which:
                    keyed(i, body)

        def first(i, keys):
            scores = nt(kv[h, 0, keys, :], queries)
            e = jnp.exp(scores * score_scale)
            if i == 0:
                e = jnp.where(col < row, e, 0.0)
            if i == BLOCKS - 1:
                e = jnp.where(col >= row, e, 0.0)
            dp = nt(kv[h, 1, keys, :], grads)
            e_b[i] = e
            d_b[i] = dp
            l_b[...] += jnp.sum(e, axis=0, keepdims=True)
            delta_b[...] += jnp.sum(e * dp, axis=0, keepdims=True)

        each((4, 3, 2), first)
        for g in range(2):
            @pl.when((s == 2 * g) & has_prev2)
            def _():
                send_on(g, 0).wait_recv()
                send_on(g, 1).wait_recv()

        each((1, 0), first)
        il = 1.0 / l_b[...]
        delta = delta_b[...] * il

        def second(i, keys):
            p = e_b[i] * il
            ds = (p * (d_b[i] - delta) * score_scale).astype(BF16)
            acc[h, 0, keys, :] += jnp.dot(ds, queries, preferred_element_type=F32)
            acc[h, 1, keys, :] += jnp.dot(p.astype(BF16), grads, preferred_element_type=F32)
            dqt[...] += tn(kv[h, 0, keys, :], ds)

        each(range(BLOCKS), second)
        dq = jnp.transpose(dqt[...])
        dq_raw, gain_part = norm_back(raw, inv, qg[...], dq)
        gain_acc[0:1, :] += gain_part
        dq_raw = dq_raw.astype(BF16)
        dq_s[s, :, 0:D] = dq_raw[0:T]
        dq_s[s, :, D : 2 * D] = dq_raw[T : 2 * T]

        @pl.when(qb == x)
        def _():
            put_local(h, s).start()

        @pl.when(qb != x)
        def _():
            put_remote(h, s).start()

    def dq_place(h):
        return dq_o.at[:, pl.ds(pl.multiple_of(x * 4 * D + h * 2 * D, 2 * D), 2 * D)]

    def put_local(h, s):
        return pltpu.make_async_copy(dq_s.at[s], dq_place(h), o_loc.at[h])

    def put_remote(h, s):
        return remote(dq_s.at[s], dq_place(h), o_snd.at[h], o_rcv.at[h], side)

    def start_two(h, half):
        @pl.when(has_prev2)
        def _():
            term[h, 0, half] = acc[h, :, half_rows(2, half), :].astype(BF16)
            back_two(h, half).start()

    def start_one(h, half):
        @pl.when(has_prev & has_next)
        def _():
            back_two(h, half).wait_recv()
            term[h, 1, half] = (acc[h, :, half_rows(1, half), :] + got[h, 0, half].astype(F32)).astype(BF16)

        @pl.when(has_prev & jnp.logical_not(has_next))
        def _():
            term[h, 1, half] = acc[h, :, half_rows(1, half), :].astype(BF16)

        @pl.when(has_prev)
        def _():
            back_one(h, half).start()

    def place(dst, h):
        return dst.at[:, pl.ds(pl.multiple_of(x * 2 * D + h * D, D), D)]

    def keep(h):
        return [pltpu.make_async_copy(src.at[h, mine], place(dst, h), p_loc.at[h, i])
                for i, (src, dst) in enumerate(((dk_s, dk_o), (dv_s, dv_o)))]

    def give(h):
        return [remote(src.at[h, theirs], place(dst, h), p_snd.at[h, i], p_rcv.at[h, i], side)
                for i, (src, dst) in enumerate(((dk_s, dk_o), (dv_s, dv_o)))]

    def finish(h, half):
        rows = pl.ds(pl.multiple_of(half * T, T), T)
        here = half_rows(0, half)

        @pl.when(has_next)
        def _():
            back_one(h, half).wait_recv()
            acc[h, :, here, :] += got[h, 1, half].astype(F32)

        raw = k_b[rows, h * D : (h + 1) * D].astype(F32)
        dk_raw, _ = norm_back(raw, inverse_norm(raw), kg[...], acc[h, 0, here, :])
        dk_s[h, rows] = dk_raw.astype(BF16)
        dv_s[h, rows] = acc[h, 1, here, :].astype(BF16)

        @pl.when(x == half)
        def _():
            for copy in keep(h):
                copy.start()

        @pl.when(x != half)
        def _():
            for copy in give(h):
                copy.start()

    def arrived(h):
        for far, near in rows_in[h]:
            near.wait()
            far.wait_recv()

    def step(s, carry):
        @pl.when(s == 0)
        def _():
            arrived(0)

        @pl.when(s == 1)
        def _():
            forward(1, x)
            forward(1, 1 - x)

        @pl.when(s == 2)
        def _():
            arrived(1)

        attend(s)

        @pl.when(s == 0)
        def _():
            start_two(0, 0)

        @pl.when(s == 1)
        def _():
            start_two(0, 1)
            start_one(0, 0)

        @pl.when(s == 2)
        def _():
            start_one(0, 1)
            start_two(1, 0)

        return carry

    lax.fori_loop(0, 4, step, 0)
    start_two(1, 1)
    start_one(1, 0)

    def key_gain(hop):
        rows = slice((4 - 2 * hop) * T, (6 - 2 * hop) * T)
        for h in range(2):
            gain_acc[1:2, :] += jnp.sum(acc[h, 0, rows, :] * kv[h, 0, rows, :].astype(F32), axis=0, keepdims=True)

    key_gain(0)
    pl.when(has_prev)(lambda: key_gain(1))
    pl.when(has_prev2)(lambda: key_gain(2))

    def spread(size, me, axis, buf, snd, rcv):
        copies = []
        for k in range(1, size):
            copies.append(remote(buf.at[me], buf.at[me], snd.at[k], rcv.at[k], {axis: lax.rem(me + k, size)}))
        for copy in copies:
            copy.start()
        return copies

    gain_c[c] = gain_acc[...]
    over_ctx = spread(n, c, "ctx", gain_c, c_snd, c_rcv)
    finish(0, 0)
    finish(0, 1)
    start_one(1, 1)
    for copy in over_ctx:
        copy.wait_recv()
    gain_t[tp] = jnp.sum(gain_c[...], axis=0)
    over_tp = spread(m, tp, "tp", gain_t, t_snd, t_rcv)
    finish(1, 0)
    finish(1, 1)
    for copy in over_tp:
        copy.wait_recv()
    total = jnp.sum(gain_t[...], axis=0)
    gain_o[0:1, :] = total[0:1] * ((n * T * Q_HEADS) ** -0.5)
    gain_o[1:2, :] = total[1:2] / kg[...] * ((n * T * KV_HEADS) ** -0.5)

    for copy in over_ctx + over_tp:
        copy.wait_send()
    for h in range(2):
        for far, _ in keys_in[h] + rows_in[h]:
            far.wait_send()
        for half in range(2):
            @pl.when(has_next)
            def _():
                send_own(h, half).wait_send()

            @pl.when(has_prev & has_next)
            def _():
                send_on(h, half).wait_send()

            @pl.when(has_prev2)
            def _():
                back_two(h, half).wait_send()

            @pl.when(has_prev)
            def _():
                back_one(h, half).wait_send()

        put_local(h, 2 * h + x).wait()
        put_remote(h, 2 * h + 1 - x).wait()
        for copy in keep(h) + give(h):
            copy.wait()


def per_device(n, m, q_raw, k_raw, v_cur, d_out, q_gain, k_gain):
    dma = pltpu.SemaphoreType.DMA
    anywhere = pl.BlockSpec(memory_space=pl.ANY)
    vmem = pl.BlockSpec(memory_space=pltpu.VMEM)
    dq_raw, dk_raw, dv, gains = pl.pallas_call(
        functools.partial(kernel, n, m),
        out_shape=(
            jax.ShapeDtypeStruct(q_raw.shape, BF16),
            jax.ShapeDtypeStruct(k_raw.shape, BF16),
            jax.ShapeDtypeStruct(v_cur.shape, BF16),
            jax.ShapeDtypeStruct((2, D), F32),
        ),
        in_specs=[pl.BlockSpec(memory_space=pltpu.HBM)] * 4 + [vmem] * 2,
        out_specs=(anywhere, anywhere, anywhere, vmem),
        scratch_shapes=[
            pltpu.VMEM((2 * T, 4 * D), BF16),
            pltpu.VMEM((2 * T, 4 * D), BF16),
            pltpu.VMEM((2 * T, 2 * D), BF16),
            pltpu.VMEM((2 * T, 2 * D), BF16),
            pltpu.VMEM((2, 2, 6 * T, D), BF16),
            pltpu.VMEM((BLOCKS, T, 2 * T), F32),
            pltpu.VMEM((BLOCKS, T, 2 * T), F32),
            pltpu.VMEM((1, 2 * T), F32),
            pltpu.VMEM((1, 2 * T), F32),
            pltpu.VMEM((D, 2 * T), F32),
            pltpu.VMEM((2, 2, 6 * T, D), F32),
            pltpu.VMEM((2, 2, 2, 2, T, D), BF16),
            pltpu.VMEM((2, 2, 2, 2, T, D), BF16),
            pltpu.VMEM((4, T, 2 * D), BF16),
            pltpu.VMEM((2, 2 * T, D), BF16),
            pltpu.VMEM((2, 2 * T, D), BF16),
            pltpu.VMEM((8, D), F32),
            pltpu.VMEM((n, 8, D), F32),
            pltpu.VMEM((m, 8, D), F32),
            dma((4, 2)), dma((4, 2)), dma((4, 2)),
            dma((2, 2, 2)), dma((2, 2, 2)), dma((2, 2, 2)), dma((2, 2, 2)),
            dma((2,)), dma((2,)), dma((2,)),
            dma((2, 2)), dma((2, 2)), dma((2, 2)),
            dma((n,)), dma((n,)), dma((m,)), dma((m,)),
        ],
        compiler_params=pltpu.CompilerParams(
            collective_id=0, has_side_effects=True, vmem_limit_bytes=63 * 1024 * 1024
        ),
    )(q_raw, k_raw, v_cur, d_out, q_gain.reshape(1, D), k_gain.reshape(1, D))
    return (dq_raw, dk_raw, dv, gains[0], gains[1])


def solution(mesh):
    return jax.shard_map(
        functools.partial(per_device, mesh.shape["ctx"], mesh.shape["tp"]),
        mesh=mesh,
        in_specs=(P("ctx", "tp"), P("ctx", "tp"), P("ctx", "tp"), P("ctx", "tp"), P(), P()),
        out_specs=(P("ctx", "tp"), P("ctx", "tp"), P("ctx", "tp"), P(), P()),
        check_vma=False,
    )
```
